32 devices in a mesh: dp: 8 (over z, y), tensor: 4 (over x, core).
Axes of the slice: x: 2, y: 2, z: 4, core: 2. Of those that a mesh axis runs over, the one named last changes fastest.
Arguments:
- hidden: bfloat16 [8192, 1024], P(('dp', 'tensor'))
- grad_query: bfloat16 [8192, 512], P('dp', 'tensor')
- grad_key: bfloat16 [8192, 512], P('dp', 'tensor')
- grad_value: bfloat16 [8192, 1024], P('dp', 'tensor')
- grad_gate: bfloat16 [8192, 1024], P('dp', 'tensor')
- attended: bfloat16 [8192, 1024], P('dp', 'tensor')
- grad_output: bfloat16 [8192, 1024], P(('dp', 'tensor'))
- owner_table: int32 [64], replicated, may hold values from 0 to 7, as said below
- left_stat: float32 [16384, 512], P('dp', 'tensor')
- right_stat: float32 [16384, 512], P('dp', 'tensor')
- left_root: float32 [16384, 512], P('dp', 'tensor')
- right_root: float32 [16384, 512], P('dp', 'tensor')
- first_moment: float32 [16384, 512], P('dp', 'tensor')
- second_moment: float32 [16384, 512], P('dp', 'tensor'), may hold values from 0.25 to 4
Outputs:
- new_left: float32 [16384, 512], P('dp', 'tensor')
- new_right: float32 [16384, 512], P('dp', 'tensor')
- new_first: float32 [16384, 512], P('dp', 'tensor')
- new_second: float32 [16384, 512], P('dp', 'tensor')
- update: float32 [64, 128, 512], P(None, 'dp', 'tensor')
The draws below stay inside these ranges and needn't reach their ends.
Inputs may be any that keep to these rules, and one draw needn't show every extreme that they name: owner_table[b] is the index of dp that owns tile b for every index of tensor; each index of dp is named by at most 16 tiles, and at least one index by exactly 16.
All inputs are finite; a program needn't handle non-finite values.
Results may differ from the reference program's by a relative error of at most 0.0029.
Values may be sent and summed in bfloat16 or wider, within the bound.
No kernel may reach another device: no remote copies, remote signals or barrier semaphores. Data moves between devices by JAX's collectives and lax.ppermute only.
A program may use at most 64 MiB of HBM per device.

```python
import math
import jax
import jax.numpy as jnp
from jax import lax

D = 1024
KEY = 512
VAL = 1024
BLK = 128
TOK_DEV = 1024
TOKENS = 8192
NBLK = 64
SLOTS = 16
N_DP = 8
N_TENSOR = 4


def activation_draw(key, row_count, col_count, scale):
    key_base = jax.random.fold_in(key, 0)
    values = jax.random.normal(key_base, (row_count, col_count), jnp.float32)
    return (scale * values).astype(jnp.bfloat16)


def cot_scale():
    return float(TOKENS) ** (-0.5)


def draw_hidden(key, part):
    return activation_draw(jax.random.fold_in(key, 11), TOKENS, D, 1.0)


def draw_grad_query(key, part):
    return activation_draw(jax.random.fold_in(key, 12), TOKENS, KEY, cot_scale())


def draw_grad_key(key, part):
    return activation_draw(jax.random.fold_in(key, 13), TOKENS, KEY, cot_scale())


def draw_grad_value(key, part):
    return activation_draw(jax.random.fold_in(key, 14), TOKENS, VAL, cot_scale())


def draw_grad_gate(key, part):
    return activation_draw(jax.random.fold_in(key, 15), TOKENS, VAL, cot_scale())


def draw_attended(key, part):
    return activation_draw(jax.random.fold_in(key, 16), TOKENS, VAL, 1.0)


def draw_grad_output(key, part):
    return activation_draw(jax.random.fold_in(key, 17), TOKENS, D, cot_scale())


def draw_owner_table(key, part):
    key_perm, key_mix = jax.random.split(jax.random.fold_in(key, 7))
    slot_total = N_DP * SLOTS
    ordering = jax.random.permutation(key_perm, slot_total).astype(jnp.int32)
    ranking = jnp.argsort(ordering).astype(jnp.int32)
    favoured = ordering[0] // SLOTS
    slot_ids = jnp.arange(slot_total, dtype=jnp.int32)
    scores = jnp.where(slot_ids // SLOTS == favoured, ranking - slot_total, ranking)
    taken = jnp.argsort(scores)[:NBLK].astype(jnp.int32)
    owners = (taken // SLOTS).astype(jnp.int32)
    mixing = jax.random.permutation(key_mix, NBLK)
    return owners[mixing].astype(jnp.int32)


def symmetric_draw(key, diag_lo, diag_hi, off_scale):
    key_diag, key_off = jax.random.split(key)
    place_total = N_DP * SLOTS
    diagonal = jnp.exp(jax.random.uniform(key_diag, (place_total, BLK, N_TENSOR, 1), jnp.float32, math.log(diag_lo), math.log(diag_hi)))
    noise = jax.random.normal(key_off, (place_total, BLK, N_TENSOR, BLK), jnp.float32)
    noise = (noise + jnp.transpose(noise, (0, 3, 2, 1))) * (off_scale / math.sqrt(2.0))
    identity = (jnp.arange(BLK)[:, None, None] == jnp.arange(BLK)[None, None, :]).astype(jnp.float32)
    matrix = noise * (1.0 - identity) + diagonal * identity
    return matrix.reshape(place_total * BLK, N_TENSOR * BLK).astype(jnp.float32)


def draw_left_stat(key, part):
    return symmetric_draw(jax.random.fold_in(key, 21), 2.0, 16.0, 0.5)


def draw_right_stat(key, part):
    return symmetric_draw(jax.random.fold_in(key, 22), 2.0, 16.0, 0.5)


def draw_left_root(key, part):
    return symmetric_draw(jax.random.fold_in(key, 23), 0.75, 1.5, 0.3 * float(BLK) ** (-0.5))


def draw_right_root(key, part):
    return symmetric_draw(jax.random.fold_in(key, 24), 0.75, 1.5, 0.3 * float(BLK) ** (-0.5))


def draw_first_moment(key, part):
    key_base = jax.random.fold_in(jax.random.fold_in(key, 31), 0)
    row_total = N_DP * SLOTS * BLK
    col_total = N_TENSOR * BLK
    row_owner = jnp.arange(row_total, dtype=jnp.int32) // (SLOTS * BLK)
    col_tensor = jnp.arange(col_total, dtype=jnp.int32) // BLK
    joint = (row_owner[:, None] * N_TENSOR + col_tensor[None, :]).astype(jnp.float32)
    rising = jnp.exp(math.log(3.0) * joint / float(max(N_DP * N_TENSOR - 1, 1)))
    values = jax.random.normal(key_base, (row_total, col_total), jnp.float32)
    return (values * rising).astype(jnp.float32)


def level_of(own_key, shape, cuts, least, top_value):
    loudness, own = 1.0, jax.random.fold_in(own_key, 6)
    for position, blocks in cuts:
        draws = jnp.exp(jax.random.uniform(jax.random.fold_in(own, position), (blocks,), jnp.float32, least / len(cuts), top_value / len(cuts)))
        loudness = loudness * jnp.repeat(draws, shape[position] // blocks).reshape([-1 if axis == position else 1 for axis in range(len(shape))])
    return loudness


def setup_inputs(seed: int = 0) -> dict:
    seeds = jax.random.split(jax.random.key(seed), 15)
    return {
        "hidden": draw_hidden(jax.random.fold_in(seeds[14], 71), 0),
        "grad_query": draw_grad_query(jax.random.fold_in(seeds[14], 71), 0),
        "grad_key": draw_grad_key(jax.random.fold_in(seeds[14], 71), 0),
        "grad_value": draw_grad_value(jax.random.fold_in(seeds[14], 71), 0),
        "grad_gate": draw_grad_gate(jax.random.fold_in(seeds[14], 71), 0),
        "attended": draw_attended(jax.random.fold_in(seeds[14], 71), 0),
        "grad_output": draw_grad_output(jax.random.fold_in(seeds[14], 71), 0),
        "owner_table": draw_owner_table(jax.random.fold_in(seeds[14], 71), 0),
        "left_stat": draw_left_stat(jax.random.fold_in(seeds[14], 71), 0),
        "right_stat": draw_right_stat(jax.random.fold_in(seeds[14], 71), 0),
        "left_root": draw_left_root(jax.random.fold_in(seeds[14], 71), 0),
        "right_root": draw_right_root(jax.random.fold_in(seeds[14], 71), 0),
        "first_moment": draw_first_moment(jax.random.fold_in(seeds[14], 71), 0),
        "second_moment": jnp.clip(jnp.exp(math.log(4.0) - 2.7725887 * jax.random.uniform(seeds[13], (N_DP * SLOTS * BLK, N_TENSOR * BLK), jnp.float32) ** level_of(seeds[13], (N_DP * SLOTS * BLK, N_TENSOR * BLK), ((0, 8), (1, 4)), -0.2, 0.2)), 0.25, 4.0),
    }


def cut_tiles(matrix):
    row_total, col_total = matrix.shape
    shaped = matrix.reshape(row_total // BLK, BLK, col_total // BLK, BLK)
    return shaped.transpose(0, 2, 1, 3).reshape(-1, BLK, BLK)

def as_places(state):
    return state.reshape(N_DP * SLOTS, BLK, N_TENSOR, BLK).transpose(0, 2, 1, 3)

def from_places(tiled):
    return tiled.transpose(0, 2, 1, 3).reshape(N_DP * SLOTS * BLK, N_TENSOR * BLK)

def grad_o_rows(grad_out, column, value_cols):
    return grad_out[column * value_cols:(column + 1) * value_cols, :]

def reference(hidden, grad_query, grad_key, grad_value, grad_gate, attended, grad_output, owner_table, left_stat, right_stat, left_root, right_root, first_moment, second_moment):
    highest = lax.Precision.HIGHEST
    cotangent = jnp.concatenate([grad_query, grad_key, grad_value, grad_gate], axis=1)
    contract = (((0,), (0,)), ((), ()))

    def accumulate(totals, data_index):
        offset = (data_index * TOK_DEV).astype(jnp.int32)
        token_block = lax.dynamic_slice_in_dim(hidden, offset, TOK_DEV, 0)
        cot_block = lax.dynamic_slice_in_dim(cotangent, offset, TOK_DEV, 0)
        att_block = lax.dynamic_slice_in_dim(attended, offset, TOK_DEV, 0)
        out_block = lax.dynamic_slice_in_dim(grad_output, offset, TOK_DEV, 0)
        part_in = lax.optimization_barrier(lax.dot_general(token_block, cot_block, contract, preferred_element_type=jnp.float32).astype(jnp.bfloat16))
        part_out = lax.optimization_barrier(lax.dot_general(att_block, out_block, contract, preferred_element_type=jnp.float32).astype(jnp.bfloat16))
        return ((totals[0] + part_in.astype(jnp.float32), totals[1] + part_out.astype(jnp.float32)), None)
    initial = (jnp.zeros((D, 2 * KEY + 2 * VAL), jnp.float32), jnp.zeros((VAL, D), jnp.float32))
    (grad_in, grad_out), _ = lax.scan(accumulate, initial, jnp.arange(N_DP, dtype=jnp.int32))
    grad_q = grad_in[:, :KEY]
    grad_k = grad_in[:, KEY:2 * KEY]
    grad_v = grad_in[:, 2 * KEY:2 * KEY + VAL]
    grad_g = grad_in[:, 2 * KEY + VAL:]
    key_cols = KEY // N_TENSOR
    value_cols = VAL // N_TENSOR
    per_column = []
    for column in range(N_TENSOR):
        pieces = [cut_tiles(grad_q[:, column * key_cols:(column + 1) * key_cols]), cut_tiles(grad_k[:, column * key_cols:(column + 1) * key_cols]), cut_tiles(grad_v[:, column * value_cols:(column + 1) * value_cols]), cut_tiles(grad_g[:, column * value_cols:(column + 1) * value_cols]), cut_tiles(grad_o_rows(grad_out, column, value_cols))]
        per_column.append(jnp.concatenate(pieces, axis=0))
    tiles = jnp.stack(per_column, axis=1)
    block_index = jnp.arange(NBLK, dtype=jnp.int32)
    earlier_same = (owner_table[:, None] == owner_table[None, :]) & (block_index[None, :] < block_index[:, None])
    slot_of = lax.optimization_barrier(jnp.sum(earlier_same.astype(jnp.int32), axis=1))
    slot_id = (owner_table * SLOTS + slot_of).astype(jnp.int32)
    query_tiles = D // BLK * (key_cols // BLK)
    value_tiles = D // BLK * (value_cols // BLK)
    boundaries = jnp.array([query_tiles, 2 * query_tiles, 2 * query_tiles + value_tiles, 2 * query_tiles + 2 * value_tiles], jnp.int32)
    matrix_of = lax.optimization_barrier(jnp.sum((block_index[:, None] >= boundaries[None, :]).astype(jnp.int32), axis=1))
    place_total = N_DP * SLOTS
    grad_tile = jnp.zeros((place_total, N_TENSOR, BLK, BLK), jnp.float32).at[slot_id].set(tiles)
    occupied = jnp.zeros((place_total,), jnp.float32).at[slot_id].set(1.0)
    place_matrix = jnp.zeros((place_total,), jnp.int32).at[slot_id].set(matrix_of)
    left_old = as_places(left_stat)
    right_old = as_places(right_stat)
    left_inv = as_places(left_root)
    right_inv = as_places(right_root)
    first_old = as_places(first_moment)
    second_old = as_places(second_moment)
    new_left = 0.95 * left_old + 0.05 * jnp.einsum('qtij,qtkj->qtik', grad_tile, grad_tile, precision=highest)
    new_right = 0.95 * right_old + 0.05 * jnp.einsum('qtji,qtjk->qtik', grad_tile, grad_tile, precision=highest)
    new_first = 0.9 * first_old + 0.1 * grad_tile
    new_second = 0.95 * second_old + 0.05 * grad_tile * grad_tile
    adam = new_first / (jnp.sqrt(new_second) + 1e-08)
    precond = jnp.einsum('qtij,qtjk->qtik', left_inv, grad_tile, precision=highest)
    precond = jnp.einsum('qtij,qtjk->qtik', precond, right_inv, precision=highest)
    adam_sums = lax.optimization_barrier(jnp.sum(adam * adam, axis=(1, 2, 3))) * occupied
    pre_sums = lax.optimization_barrier(jnp.sum(precond * precond, axis=(1, 2, 3))) * occupied
    one_hot = (place_matrix[:, None] == jnp.arange(5, dtype=jnp.int32)[None, :]).astype(jnp.float32)
    sum_adam = lax.optimization_barrier(jnp.sum(one_hot * adam_sums[:, None], axis=0))
    sum_pre = lax.optimization_barrier(jnp.sum(one_hot * pre_sums[:, None], axis=0))
    counts = jnp.array([D * KEY, D * KEY, D * VAL, D * VAL, VAL * D], jnp.float32)
    graft_scale = jnp.sqrt(sum_adam / counts / (sum_pre / counts + 1e-06))
    chosen = precond[slot_id] * graft_scale[matrix_of][:, None, None, None]
    update = chosen.transpose(0, 2, 1, 3).reshape(NBLK, BLK, N_TENSOR * BLK)
    return (from_places(new_left), from_places(new_right), from_places(new_first), from_places(new_second), update)
```

```python
import functools
import jax
import jax.numpy as jnp
import numpy as np
from jax import lax
from jax.experimental import pallas as pl
from jax.experimental.pallas import tpu as pltpu
from jax.sharding import PartitionSpec as P

D = 1024
KEY = 512
VAL = 1024
BLK = 128
HIGHEST = lax.Precision.HIGHEST
CONTRACT_ROWS = (((0,), (0,)), ((), ()))


def swap(array, axis, bit):
    size = lax.axis_size(axis)
    return lax.ppermute(array, axis, [(i, i ^ bit) for i in range(size)])


def gather_blocks(block, axis):
    found = {0: block}
    bit = lax.axis_size(axis) // 2
    while bit:
        for offset in sorted(found):
            found[offset ^ bit] = swap(found[offset], axis, bit)
        bit //= 2
    return [found[offset] for offset in sorted(found)]


def spread_rows(acc, out, pieces):
    rows = BLK // pieces
    for tile_row in range(acc.shape[0] // BLK):
        for tile_col in range(acc.shape[1] // BLK):
            for piece in range(pieces):
                top = tile_row * BLK + piece * rows
                out[piece, tile_row, tile_col] = acc[
                    top : top + rows, tile_col * BLK : (tile_col + 1) * BLK
                ]


def input_kernel(pieces, own, *refs):
    blocks, (query, key, value, gate, out) = refs[:-5], refs[-5:]
    tokens = blocks[0].shape[0]
    acc = None
    for offset, block in enumerate(blocks):
        rows = pl.ds(pl.multiple_of((own[0] ^ offset) * tokens, tokens), tokens)
        right = jnp.concatenate([query[rows], key[rows], value[rows], gate[rows]], axis=1)
        term = lax.dot_general(
            block[...], right, CONTRACT_ROWS, preferred_element_type=jnp.float32
        )
        acc = term if acc is None else acc + term
    spread_rows(acc.astype(jnp.bfloat16), out, pieces)


def output_kernel(pieces, own, *refs):
    blocks, (left, out) = refs[:-2], refs[-2:]
    tokens = blocks[0].shape[0]
    acc = None
    for offset, block in enumerate(blocks):
        rows = pl.ds(pl.multiple_of((own[0] ^ offset) * tokens, tokens), tokens)
        term = lax.dot_general(
            left[rows], block[...], CONTRACT_ROWS, preferred_element_type=jnp.float32
        )
        acc = term if acc is None else acc + term
    spread_rows(acc.astype(jnp.bfloat16), out, pieces)


def whole(array):
    return pl.BlockSpec(array.shape, lambda *_: (0,) * array.ndim)


def input_partials(own, blocks, cotangents, pieces):
    tokens, width = blocks[0].shape
    step = 2 * BLK
    tile_cols = sum(c.shape[1] for c in cotangents) // BLK
    rows = BLK // pieces
    if rows % 16:
        parts = [c.reshape(len(blocks), tokens, -1) for c in cotangents]
        right = jnp.concatenate(parts, axis=2)
        right = jnp.take(right, own ^ jnp.arange(len(blocks)), axis=0)
        acc = lax.dot_general(
            jnp.concatenate(blocks, axis=0),
            right.reshape(-1, right.shape[2]),
            CONTRACT_ROWS,
            preferred_element_type=jnp.float32,
        ).astype(jnp.bfloat16)
        return plain_spread(acc, pieces)
    return pl.pallas_call(
        functools.partial(input_kernel, pieces),
        out_shape=jax.ShapeDtypeStruct(
            (pieces, width // BLK, tile_cols, rows, BLK), jnp.bfloat16
        ),
        grid=(width // step,),
        in_specs=[pl.BlockSpec(memory_space=pltpu.SMEM)]
        + [pl.BlockSpec((tokens, step), lambda i: (0, i)) for _ in blocks]
        + [whole(c) for c in cotangents],
        out_specs=pl.BlockSpec(
            (pieces, step // BLK, tile_cols, rows, BLK), lambda i: (0, i, 0, 0, 0)
        ),
        cost_estimate=pl.CostEstimate(
            flops=2 * len(blocks) * tokens * width * tile_cols * BLK,
            bytes_accessed=6 * 1024 * 1024,
            transcendentals=0,
        ),
    )(own.reshape(1), *blocks, *cotangents)


def output_partials(own, blocks, left, pieces):
    tokens, width = blocks[0].shape
    step = 2 * BLK
    tile_rows = left.shape[1] // BLK
    rows = BLK // pieces
    if rows % 16:
        lefts = jnp.take(
            left.reshape(len(blocks), tokens, -1), own ^ jnp.arange(len(blocks)), axis=0
        )
        acc = lax.dot_general(
            lefts.reshape(-1, left.shape[1]),
            jnp.concatenate(blocks, axis=0),
            CONTRACT_ROWS,
            preferred_element_type=jnp.float32,
        ).astype(jnp.bfloat16)
        return plain_spread(acc, pieces)
    return pl.pallas_call(
        functools.partial(output_kernel, pieces),
        out_shape=jax.ShapeDtypeStruct(
            (pieces, tile_rows, width // BLK, rows, BLK), jnp.bfloat16
        ),
        grid=(width // step,),
        in_specs=[pl.BlockSpec(memory_space=pltpu.SMEM)]
        + [pl.BlockSpec((tokens, step), lambda i: (0, i)) for _ in blocks]
        + [whole(left)],
        out_specs=pl.BlockSpec(
            (pieces, tile_rows, step // BLK, rows, BLK), lambda i: (0, 0, i, 0, 0)
        ),
        cost_estimate=pl.CostEstimate(
            flops=2 * len(blocks) * tokens * width * tile_rows * BLK,
            bytes_accessed=3 * 1024 * 1024,
            transcendentals=0,
        ),
    )(own.reshape(1), *blocks, left)


def plain_spread(acc, pieces):
    shaped = acc.reshape(acc.shape[0] // BLK, pieces, BLK // pieces, acc.shape[1] // BLK, BLK)
    return shaped.transpose(1, 0, 3, 2, 4)


def exchange(array, axis):
    return lax.all_to_all(array, axis, 0, 0, tiled=True)


def exchange_order(key_cols, value_cols):
    key_c, value_c = key_cols // BLK, value_cols // BLK
    tile_cols = 2 * key_c + 2 * value_c
    order = []
    start = 0
    for count in (key_c, key_c, value_c, value_c):
        for tile_row in range(D // BLK):
            for col in range(count):
                order.append(tile_row * tile_cols + start + col)
        start += count
    return np.array(order + list(range(len(order), len(order) + value_c * (D // BLK))), np.int32)


def shards(
    hidden,
    grad_query,
    grad_key,
    grad_value,
    grad_gate,
    attended,
    grad_output,
    owner_table,
    left_stat,
    right_stat,
    left_root,
    right_root,
    first_moment,
    second_moment,
):
    data_size = lax.axis_size("dp")
    own_index = lax.axis_index("dp")
    column = lax.axis_index("tensor").astype(jnp.int32)
    key_cols = grad_query.shape[1]
    value_cols = grad_value.shape[1]
    rows = BLK // data_size

    hidden_blocks = gather_blocks(hidden, "tensor")
    out_blocks = gather_blocks(grad_output, "tensor")
    part_in = input_partials(
        column, hidden_blocks, (grad_query, grad_key, grad_value, grad_gate), data_size
    )
    part_in = exchange(part_in, "dp")
    part_out = output_partials(column, out_blocks, attended, data_size)
    part_out = exchange(part_out, "dp")

    block_count = owner_table.shape[0]
    slot_count = left_stat.shape[0] // BLK
    block_index = jnp.arange(block_count, dtype=jnp.int32)
    earlier_same = (owner_table[:, None] == owner_table[None, :]) & (
        block_index[None, :] < block_index[:, None]
    )
    slot_of = jnp.sum(earlier_same.astype(jnp.int32), axis=1)
    slot_id = owner_table * slot_count + slot_of
    query_tiles = D // BLK * (key_cols // BLK)
    value_tiles = D // BLK * (value_cols // BLK)
    boundaries = np.array(
        [
            query_tiles,
            2 * query_tiles,
            2 * query_tiles + value_tiles,
            2 * query_tiles + 2 * value_tiles,
        ],
        np.int32,
    )
    matrix_of = np.sum(
        np.arange(block_count)[:, None] >= boundaries[None, :], axis=1
    ).astype(np.int32)
    order = jnp.asarray(exchange_order(key_cols, value_cols))
    place_ids = jnp.arange(data_size * slot_count, dtype=jnp.int32)
    hits = slot_id[None, :] == place_ids[:, None]
    source = jnp.sum(jnp.where(hits, order[None, :], 0), axis=1)
    present = jnp.any(hits, axis=1)
    own_places = own_index * slot_count + jnp.arange(slot_count, dtype=jnp.int32)
    own_hits = slot_id[None, :] == own_places[:, None]
    member = own_hits[:, :, None] & (
        jnp.asarray(matrix_of)[None, :, None] == jnp.arange(5, dtype=jnp.int32)[None, None, :]
    )
    one_hot = jnp.sum(member.astype(jnp.float32), axis=1)

    sum_in = jnp.sum(part_in.astype(jnp.float32), axis=0).reshape(-1, rows, BLK)
    sum_out = jnp.sum(part_out.astype(jnp.float32), axis=0).reshape(-1, rows, BLK)
    row_sums = jnp.concatenate([sum_in, sum_out], axis=0).astype(jnp.bfloat16)
    packed = jnp.where(present[:, None, None], jnp.take(row_sums, source, axis=0), 0)
    received = exchange(packed, "dp").reshape(data_size, slot_count, rows, BLK)
    owned = received.transpose(1, 0, 2, 3).reshape(slot_count, BLK, BLK).astype(jnp.float32)

    tile_shape = (slot_count, BLK, BLK)
    left_old = left_stat.reshape(tile_shape)
    right_old = right_stat.reshape(tile_shape)
    left_inv = left_root.reshape(tile_shape)
    right_inv = right_root.reshape(tile_shape)
    first_old = first_moment.reshape(tile_shape)
    second_old = second_moment.reshape(tile_shape)
    precond = jnp.einsum("sij,sjk->sik", left_inv, owned, precision=HIGHEST)
    precond = jnp.einsum("sij,sjk->sik", precond, right_inv, precision=HIGHEST)
    returned = exchange(
        precond.astype(jnp.bfloat16)
        .reshape(slot_count, data_size, rows, BLK)
        .transpose(1, 0, 2, 3)
        .reshape(data_size * slot_count, rows, BLK),
        "dp",
    )
    new_first = 0.9 * first_old + 0.1 * owned
    new_second = 0.95 * second_old + 0.05 * owned * owned
    adam = new_first / (jnp.sqrt(new_second) + 1e-08)
    adam_sums = jnp.sum(adam * adam, axis=(1, 2))
    pre_sums = jnp.sum(precond * precond, axis=(1, 2))
    stats = jnp.concatenate(
        [
            jnp.sum(one_hot * adam_sums[:, None], axis=0),
            jnp.sum(one_hot * pre_sums[:, None], axis=0),
        ]
    )
    device_count = data_size * lax.axis_size("tensor")
    stats = jnp.pad(stats, (0, BLK - 10))
    stats = exchange(jnp.broadcast_to(stats[None, None], (device_count, 8, BLK)), ("dp", "tensor"))
    stats = jnp.sum(stats[:, 0], axis=0)
    sum_adam, sum_pre = stats[:5], stats[5:10]
    new_left = 0.95 * left_old + 0.05 * jnp.einsum("sij,skj->sik", owned, owned, precision=HIGHEST)
    new_right = 0.95 * right_old + 0.05 * jnp.einsum(
        "sji,sjk->sik", owned, owned, precision=HIGHEST
    )
    counts = jnp.array([D * KEY, D * KEY, D * VAL, D * VAL, VAL * D], jnp.float32)
    graft_scale = jnp.sqrt(sum_adam / counts / (sum_pre / counts + 1e-06))
    tile_scale = jnp.take(graft_scale, jnp.asarray(matrix_of))
    update_rows = jnp.take(returned, slot_id, axis=0).astype(jnp.float32)
    update_rows = update_rows * tile_scale[:, None, None]
    flat_shape = (slot_count * BLK, BLK)
    return (
        new_left.reshape(flat_shape),
        new_right.reshape(flat_shape),
        new_first.reshape(flat_shape),
        new_second.reshape(flat_shape),
        update_rows,
    )


def solution(mesh):
    placed = (
        P(("dp", "tensor"), None),
        P("dp", "tensor"),
        P("dp", "tensor"),
        P("dp", "tensor"),
        P("dp", "tensor"),
        P("dp", "tensor"),
        P(("dp", "tensor"), None),
        P(),
        P("dp", "tensor"),
        P("dp", "tensor"),
        P("dp", "tensor"),
        P("dp", "tensor"),
        P("dp", "tensor"),
        P("dp", "tensor"),
    )
    return jax.shard_map(
        shards,
        mesh=mesh,
        in_specs=placed,
        out_specs=(
            P("dp", "tensor"),
            P("dp", "tensor"),
            P("dp", "tensor"),
            P("dp", "tensor"),
            P(None, "dp", "tensor"),
        ),
        check_vma=False,
    )
```
